32 devices in a mesh: rve: 2 (over x), sub: 16 (over z, y, core).
Axes of the slice: x: 2, y: 2, z: 4, core: 2. Of those that a mesh axis runs over, the one named last changes fastest.
Arguments:
- condensed: float32 [49152, 1536], P(('rve', 'sub')), parts along dimension 0, may hold values from -0.15625 to 0.15625
- eigen_loads: float32 [49152, 128], P(('rve', 'sub')), parts along dimension 0, may hold values from -6 to 6
- coarse_inverse: float32 [1536, 768], P(('rve', 'sub')), parts along dimension 0, may hold values from -0.21875 to 0.21875
- face_rows: int32 [16, 2, 128], P('sub'), may hold values from 0 to 1535, as said below
- primal_rows: int32 [16, 96], P('sub'), may hold values from 0 to 1535, as said below
- primal_slot: int32 [16, 96], P('sub'), may hold values from 0 to 95, each once within a row
Outputs:
- displaced: float32 [49152, 128], P(('rve', 'sub')), parts along dimension 0
- multipliers: float32 [4096, 128], P(('rve', 'sub')), parts along dimension 0
The draws below stay inside these ranges and needn't reach their ends.
There are 2 independent parts, one for each index of `rve`. The reference program is written for one: setup_inputs(seed, part) draws one part's arguments, and reference() takes and returns one part's arrays. A program takes and returns all parts, laid end to end along the dimension named above; an argument that names none is the same for every part. Nothing has to cross between parts.
Inputs may be any that keep to these rules, and one draw needn't show every extreme that they name: `face_rows`: in each subdomain the 128 left-face rows, the 128 right-face rows and the 96 primal rows in primal_rows are all distinct. `primal_rows`: distinct from that subdomain's face rows.
All inputs are finite; a program needn't handle non-finite values.
Results may differ from the reference program's by a relative error of at most 0.0001.
Values sent between devices are 32-bit elements; how exact they have to be, the bound alone decides.
A program may use at most 64 MiB of HBM per device.

```python
import jax
import jax.numpy as jnp
from jax import lax

B = 1536
PR = 96
IF = 128
COLS = 128
ITERS = 3
PC = 48
SUBS = 16
NC = 768


def layout_rows(key):
    keys = jax.random.split(jax.random.fold_in(key, 11), SUBS)
    return jax.vmap(lambda item: jax.random.permutation(item, B))(keys)


def draw_face_rows(key, part):
    perms = layout_rows(key)
    return perms[:, :2 * IF].reshape(SUBS, 2, IF).astype(jnp.int32)


def draw_primal_rows(key, part):
    perms = layout_rows(key)
    return perms[:, 2 * IF:2 * IF + PR].astype(jnp.int32)


def level_of(own_key, extent, cuts, smallest, largest):
    factor_of = 1.0
    for position, parts in cuts:
        draws = jax.random.uniform(jax.random.fold_in(jax.random.fold_in(own_key, 6), position), (parts,), jnp.float32, smallest / len(cuts), largest / len(cuts))
        factor_of = factor_of * jnp.repeat(jnp.exp(draws), extent[position] // parts).reshape((-1,) + (1,) * (len(extent) - 1 - position))
    return factor_of


def normal_values(own_key, dims, spread, bound, cuts=(), held_as=jnp.bfloat16):
    level = level_of(own_key, dims, cuts, -0.22, 0.18) if cuts else 1.0
    array = jax.random.normal(own_key, dims, jnp.float32) * spread * level
    return jnp.minimum(jnp.maximum(array, -bound), bound).astype(held_as)


def setup_inputs(seed: int = 0, part: int = 0) -> dict:
    key_list = jax.random.split(jax.random.key(seed), 7)
    part_splits = jax.random.split(jax.random.fold_in(key_list[6], part), 7)
    return {
        "condensed": normal_values(part_splits[0], (SUBS * B, B), B ** -0.5, 0.15625, ((0, 16),), jnp.float32),
        "eigen_loads": normal_values(part_splits[1], (SUBS * B, COLS), 1.0, 6.0, ((0, 16),), jnp.float32),
        "coarse_inverse": normal_values(part_splits[2], (NC, NC), NC ** -0.5, 0.21875, ((0, 16),), jnp.float32),
        "face_rows": draw_face_rows(jax.random.fold_in(key_list[6], 71), part),
        "primal_rows": draw_primal_rows(jax.random.fold_in(key_list[6], 71), part),
        "primal_slot": jax.vmap(lambda own: jax.random.permutation(own, PR))(jax.random.split(key_list[5], SUBS)).reshape((SUBS, PR)).astype(jnp.int32),
    }


DAMPING = 0.5


def add_faces(loads, right_rows, left_rows, right_term, left_term):
    return loads.at[right_rows].add(-right_term).at[left_rows].add(left_term)


def place_slots(values, slots):
    return jnp.zeros((PR, values.shape[1]), jnp.float32).at[slots].set(values)


def reference(condensed, eigen_loads, coarse_inverse, face_rows, primal_rows, primal_slot):
    blocks = condensed.reshape(SUBS, B, B)
    loads_all = eigen_loads.reshape(SUBS, B, COLS)
    left_rows = face_rows[:, 0, :]
    right_rows = face_rows[:, 1, :]
    prolong = jnp.take_along_axis(blocks, primal_rows[:, None, :], 2)
    multipliers = jnp.zeros((SUBS, IF, COLS), jnp.float32)
    displaced = loads_all
    for step in range(ITERS):
        previous = jnp.roll(multipliers, 1, axis=0)
        loads = jax.vmap(add_faces)(loads_all, right_rows, left_rows, multipliers, previous)
        displaced = jnp.einsum("sij,sjc->sic", blocks, loads, precision=lax.Precision.HIGHEST)
        picked = jnp.take_along_axis(displaced, primal_rows[:, :, None], 1)
        slotted = jax.vmap(place_slots)(picked, primal_slot)
        assembled = slotted[:, :PC] + jnp.roll(slotted[:, PC:], 1, axis=0)
        coarse_sol = jnp.dot(coarse_inverse, assembled.reshape(NC, COLS), precision=lax.Precision.HIGHEST, preferred_element_type=jnp.float32).reshape(SUBS, PC, COLS)
        paired = jnp.concatenate([coarse_sol, jnp.roll(coarse_sol, -1, axis=0)], axis=1)
        gathered = jnp.take_along_axis(paired, primal_slot[:, :, None], 1)
        displaced = displaced - jnp.einsum("sij,sjc->sic", prolong, gathered, precision=lax.Precision.HIGHEST)
        right_vals = jnp.take_along_axis(displaced, right_rows[:, :, None], 1)
        left_vals = jnp.take_along_axis(displaced, left_rows[:, :, None], 1)
        multipliers = multipliers + DAMPING * (right_vals - jnp.roll(left_vals, -1, axis=0))
    return displaced.reshape(SUBS * B, COLS), multipliers.reshape(SUBS * IF, COLS)
```

```python
import functools

import jax
import jax.numpy as jnp
from jax import lax
from jax.experimental import pallas as pl
from jax.experimental.pallas import tpu as pltpu
from jax.sharding import PartitionSpec as P

ITERS = 3
DAMPING = 0.5
MESH = pl.DeviceIdType.MESH
F32 = jnp.float32
BF16 = jnp.bfloat16
LANES = 128


def grid_of(count):
    chips = count // 2
    inner = 1
    while (2 * inner) ** 2 <= chips and chips % (2 * inner) == 0:
        inner *= 2
    return chips // inner, inner


def flipped(index, mask, count):
    if count & (count - 1):
        return lax.rem(index + count - mask, count)
    out = 0
    bit = 1
    while bit < count:
        own = lax.rem(index // bit, 2)
        out = out + bit * ((1 - own) if mask & bit else own)
        bit *= 2
    return out


def returned(index, mask, count):
    if count & (count - 1):
        return lax.rem(index + mask, count)
    return flipped(index, mask, count)


def split(value):
    high = value.astype(BF16)
    return high, (value - high.astype(F32)).astype(BF16)


def product(high, low, value):
    value_high, value_low = split(value)
    return product_parts(high, low, value_high, value_low)


def product_parts(high, low, value_high, value_low):
    width = value_high.shape[1]
    both = jnp.dot(high, jnp.concatenate([value_high, value_low], axis=1), preferred_element_type=F32)
    return both[:, :width] + both[:, width:] + jnp.dot(low, value_high, preferred_element_type=F32)


def kernel(
    count, primal, width, ids_s, ids_v, k_hbm, f_ref, cinv_ref, u_ref, lam_ref,
    k_ref, kh_ref, kl_ref, e_ref, fh_ref, fl_ref, ks_ref, ah_ref, al_ref, cols_ref, ch_ref, cl_ref,
    kph_ref, kpl_ref, pre_ref, gat_ref, r_ref, send_r, send_l, got_r, got_l, send_ar, send_al, got_ar, got_al,
    k_sem, send_sem, block_sem, face_sem, cinv_send, cinv_recv, a_send, a_recv,
):
    outer, inner = grid_of(count)
    order, columns = f_ref.shape
    owned = primal // 2
    tile = order // k_sem.shape[0]
    padded = e_ref.shape[1]
    me = lax.axis_index("sub")
    core = lax.rem(me, 2)
    y = lax.rem(me // 2, inner)
    z = me // (2 * inner)

    def at(z_, y_, core_):
        return (z_ * inner + y_) * 2 + core_

    def around(steps):
        return lax.rem(me + (steps + count), count)

    def k_copy(c):
        rows = pl.ds(c * tile, tile)
        return pltpu.make_async_copy(k_hbm.at[rows, :], k_ref.at[rows, :], k_sem.at[c])

    for c in range(k_sem.shape[0]):
        k_copy(c).start()

    outer_peers = [at(flipped(z, m, outer), y, core) for m in range(1, outer)]
    outer_back = [returned(z, m, outer) for m in range(1, outer)]
    inner_peers = [at(z, flipped(y, m, inner), core) for m in range(1, inner)]
    partner = at(z, y, 1 - core)
    ring = [around(d) for d in (-2, -1, 1, 2)]

    barrier = pltpu.get_barrier_semaphore()
    greeted = outer_peers + inner_peers + [partner] + ring
    if outer & (outer - 1):
        greeted = greeted + [at(b, y, core) for b in outer_back]
    for peer in greeted:
        pl.semaphore_signal(barrier, inc=1, device_id={"sub": peer}, device_id_type=MESH)
    pl.semaphore_wait(barrier, len(greeted))

    def remote(src, dst, ssem, rsem, peer):
        return pltpu.make_async_remote_copy(
            src_ref=src, dst_ref=dst, send_sem=ssem, recv_sem=rsem, device_id={"sub": peer}, device_id_type=MESH
        )

    cinv_copies = [
        remote(cinv_ref, cols_ref.at[slot], cinv_send.at[slot], cinv_recv.at[slot], around(d))
        for slot, d in ((0, 1), (1, -1), (2, -2))
    ]
    for copy in cinv_copies:
        copy.start()

    for c in range(order // tile):
        rows = lax.broadcasted_iota(jnp.int32, (tile, padded), 0) + c * tile
        e_ref[c * tile:(c + 1) * tile, :] = jnp.where(rows == ids_v[...], 1.0, 0.0).astype(BF16)
    fh, fl = split(f_ref[...])
    fh_ref[...] = fh
    fl_ref[...] = fl

    for c in range(k_sem.shape[0]):
        k_copy(c).wait()

    used = 2 * width + primal
    if padded > used:
        ks_ref[used:, :] = jnp.zeros((padded - used, order), F32)

    @pl.loop(0, used // 8)
    def _(i):
        base = pl.multiple_of(i * 8, 8)
        for j in range(8):
            ks_ref[pl.ds(base + j, 1), :] = k_ref[pl.ds(ids_s[0, base + j], 1), :]

    ksh, ksl = split(ks_ref[...])
    first = product_parts(ksh, ksl, fh_ref[...], fl_ref[...])

    def finish_a():
        high, low = split(ks_ref[...])
        a_high = jnp.dot(high, e_ref[...], preferred_element_type=F32)
        a_low = jnp.dot(low, e_ref[...], preferred_element_type=F32)
        ah_ref[...] = a_high.astype(BF16)
        al_ref[...] = a_low.astype(BF16)
        corner = (a_high + a_low)[:2 * width, 2 * width:]
        send_ar[...] = corner[:width]
        send_al[...] = corner[width:]

    def split_k():
        @pl.loop(0, order // tile)
        def _(c):
            rows = pl.ds(pl.multiple_of(c * tile, tile), tile)
            high, low = split(k_ref[rows, :])
            kh_ref[rows, :] = high
            kl_ref[rows, :] = low

    def primal_columns():
        picks = e_ref[:, 2 * width:]

        @pl.loop(0, order // tile)
        def _(c):
            rows = pl.ds(pl.multiple_of(c * tile, tile), tile)
            kph_ref[rows, :] = jnp.dot(kh_ref[rows, :], picks, preferred_element_type=F32).astype(BF16)
            kpl_ref[rows, :] = jnp.dot(kl_ref[rows, :], picks, preferred_element_type=F32).astype(BF16)

    def uncorrected(changes):
        high, low = split(changes)
        spread = jnp.dot(e_ref[:, :2 * width], jnp.concatenate([high, low], axis=1), preferred_element_type=F32)
        loads = f_ref[...] + (spread[:, :columns] + spread[:, columns:])
        high, low = split(loads)
        fh_ref[...] = high
        fl_ref[...] = low

        @pl.loop(0, order // tile)
        def _(c):
            rows = pl.ds(pl.multiple_of(c * tile, tile), tile)
            pre_ref[rows, :] = product_parts(kh_ref[rows, :], kl_ref[rows, :], fh_ref[...], fl_ref[...])

    a_copies = [
        remote(send_al, got_al, a_send.at[0], a_recv.at[0], around(-1)),
        remote(send_ar, got_ar, a_send.at[1], a_recv.at[1], around(1)),
    ]

    lam = jnp.zeros((width, columns), F32)
    lam_before = jnp.zeros((width, columns), F32)
    values = first
    changes = None
    for step in range(ITERS):
        if step:
            changes = jnp.concatenate([-lam, lam_before], axis=0)
            values = first + product(ah_ref[:, :2 * width], al_ref[:, :2 * width], changes)
        gat = gat_ref.at[step]
        gat_ref[step, me] = values[2 * width:2 * width + primal]
        send_r[step] = values[:width]
        send_l[step] = values[width:2 * width]
        started = []

        def forward(block, peer):
            copy = remote(
                gat.at[block], gat.at[block], send_sem.at[step, len(started)], block_sem.at[step, block], peer
            )
            copy.start()
            started.append(copy)

        def arrived(block):
            remote(gat.at[block], gat.at[block], send_sem.at[step, 0], block_sem.at[step, block], partner).wait_recv()

        for peer in reversed(outer_peers):
            forward(me, peer)
        for peer in inner_peers:
            forward(me, peer)
        forward(me, partner)
        faces = [
            remote(send_l.at[step], got_l.at[step], face_sem.at[0, step, 0], face_sem.at[1, step, 0], around(-1)),
            remote(send_r.at[step], got_r.at[step], face_sem.at[0, step, 1], face_sem.at[1, step, 1], around(1)),
        ]
        for copy in faces:
            copy.start()

        if step == 0:
            finish_a()
            for copy in a_copies:
                copy.start()
        if step == 1:
            primal_columns()
        if step == ITERS - 1:
            uncorrected(changes)

        for source in outer_back:
            block = at(source, y, core)
            arrived(block)
            for peer in inner_peers:
                forward(block, peer)
            forward(block, partner)
        if step == 0:
            split_k()
            for copy in cinv_copies:
                copy.wait()
            for slot, part in enumerate((cols_ref.at[0], cinv_ref, cols_ref.at[1], cols_ref.at[2])):
                high, low = split(part[...])
                ch_ref[slot * owned:(slot + 1) * owned, :] = high
                cl_ref[slot * owned:(slot + 1) * owned, :] = low
        for m in range(1, inner):
            for source in [z] + outer_back:
                block = at(source, returned(y, m, inner), core)
                arrived(block)
                forward(block, partner)
        for source in [z] + outer_back:
            for m in range(inner):
                arrived(at(source, y if m == 0 else returned(y, m, inner), 1 - core))

        for s in range(count):
            r_ref[s * owned:(s + 1) * owned, :] = (
                gat_ref[step, s, :owned, :] + gat_ref[step, (s - 1) % count, owned:, :]
            )
        coarse = product(ch_ref[...], cl_ref[...], r_ref[...])
        fill = jnp.zeros((padded - 2 * width - primal, columns), F32)

        def steps_of(slot):
            return jnp.concatenate([coarse[slot * owned:(slot + 2) * owned], fill], axis=0)

        q_before, q_own, q_after = steps_of(0), steps_of(1), steps_of(2)
        own = product(ah_ref[:2 * width, 2 * width:], al_ref[:2 * width, 2 * width:], q_own)
        if step == 0:
            for copy in a_copies:
                copy.wait()
        for copy in faces:
            copy.wait()
        after = product(*split(got_al[...]), q_after)
        lam = lam + DAMPING * ((values[:width] - own[:width]) - (got_l[step] - after))
        if step + 1 < ITERS:
            before = product(*split(got_ar[...]), q_before)
            lam_before = lam_before + DAMPING * ((got_r[step] - before) - (values[width:2 * width] - own[width:]))
        else:
            lam_ref[...] = lam
            q_high, q_low = split(q_own)

            @pl.loop(0, order // tile)
            def _(c):
                rows = pl.ds(pl.multiple_of(c * tile, tile), tile)
                u_ref[rows, :] = pre_ref[rows, :] - product_parts(kph_ref[rows, :], kpl_ref[rows, :], q_high, q_low)
        for copy in started:
            copy.wait_send()


def local(condensed, eigen_loads, coarse_inverse, face_rows, primal_rows, primal_slot):
    count = lax.axis_size("sub")
    order, columns = eigen_loads.shape
    owned, total = coarse_inverse.shape
    width = face_rows.shape[2]
    primal = primal_rows.shape[1]
    padded = 2 * width + -(-primal // LANES) * LANES
    outer, inner = grid_of(count)
    slots = lax.broadcasted_iota(jnp.int32, (primal, primal), 0)
    ordered = jnp.sum(jnp.where(primal_slot == slots, primal_rows, 0), axis=1)
    fill = jnp.full((padded - 2 * width - primal,), -1, jnp.int32)
    ids = jnp.concatenate([face_rows[0, 1], face_rows[0, 0], ordered, fill])[None]
    tile = 256 if order % 256 == 0 else order
    sends = (outer - 1) + (inner - 1) * outer + outer * inner
    dma = pltpu.SemaphoreType.DMA
    vmem = pl.BlockSpec(memory_space=pltpu.VMEM)
    face = pltpu.VMEM((ITERS, width, columns), F32)
    corner = pltpu.VMEM((width, padded - 2 * width), F32)
    return pl.pallas_call(
        functools.partial(kernel, count, primal, width),
        out_shape=(
            jax.ShapeDtypeStruct((order, columns), F32),
            jax.ShapeDtypeStruct((width, columns), F32),
        ),
        in_specs=[pl.BlockSpec(memory_space=pltpu.SMEM), vmem, pl.BlockSpec(memory_space=pl.ANY), vmem, vmem],
        out_specs=(vmem, vmem),
        scratch_shapes=[
            pltpu.VMEM((order, order), F32),
            pltpu.VMEM((order, order), BF16),
            pltpu.VMEM((order, order), BF16),
            pltpu.VMEM((order, padded), BF16),
            pltpu.VMEM((order, columns), BF16),
            pltpu.VMEM((order, columns), BF16),
            pltpu.VMEM((padded, order), F32),
            pltpu.VMEM((padded, padded), BF16),
            pltpu.VMEM((padded, padded), BF16),
            pltpu.VMEM((3, owned, total), F32),
            pltpu.VMEM((4 * owned, total), BF16),
            pltpu.VMEM((4 * owned, total), BF16),
            pltpu.VMEM((order, padded - 2 * width), BF16),
            pltpu.VMEM((order, padded - 2 * width), BF16),
            pltpu.VMEM((order, columns), F32),
            pltpu.VMEM((ITERS, count, primal, columns), F32),
            pltpu.VMEM((total, columns), F32),
            face, face, face, face,
            corner, corner, corner, corner,
            dma((order // tile,)),
            dma((ITERS, sends)),
            dma((ITERS, count)),
            dma((2, ITERS, 2)),
            dma((3,)),
            dma((3,)),
            dma((2,)),
            dma((2,)),
        ],
        compiler_params=pltpu.CompilerParams(
            collective_id=0, has_side_effects=True, vmem_limit_bytes=67043328
        ),
    )(ids, ids, condensed, eigen_loads, coarse_inverse)


def solution(mesh):
    placed = (
        P(("rve", "sub"), None),
        P(("rve", "sub"), None),
        P(("rve", "sub"), None),
        P("sub", None, None),
        P("sub", None),
        P("sub", None),
    )
    return jax.shard_map(
        local,
        mesh=mesh,
        in_specs=placed,
        out_specs=(P(("rve", "sub"), None), P(("rve", "sub"), None)),
        check_vma=False,
    )
```

```python
import functools

import jax
import jax.numpy as jnp
from jax import lax
from jax.experimental import pallas as pl
from jax.experimental.pallas import tpu as pltpu
from jax.sharding import PartitionSpec as P

ITERS = 3
DAMPING = 0.5
VMEM_LIMIT = 67043328
MESH = pl.DeviceIdType.MESH
F32 = jnp.float32
BF16 = jnp.bfloat16
LANES = 128


def grid_of(count):
    chips = count // 2
    inner = 1
    while (2 * inner) ** 2 <= chips and chips % (2 * inner) == 0:
        inner *= 2
    return chips // inner, inner


def flipped(index, mask, count):
    if count & (count - 1):
        return lax.rem(index + count - mask, count)
    out = 0
    bit = 1
    while bit < count:
        own = lax.rem(index // bit, 2)
        out = out + bit * ((1 - own) if mask & bit else own)
        bit *= 2
    return out


def returned(index, mask, count):
    if count & (count - 1):
        return lax.rem(index + mask, count)
    return flipped(index, mask, count)


def split(value):
    high = value.astype(BF16)
    return high, (value - high.astype(F32)).astype(BF16)


def product(high, low, value):
    value_high, value_low = split(value)
    return product_parts(high, low, value_high, value_low)


def product_parts(high, low, value_high, value_low):
    width = value_high.shape[1]
    both = jnp.dot(high, jnp.concatenate([value_high, value_low], axis=1), preferred_element_type=F32)
    return both[:, :width] + both[:, width:] + jnp.dot(low, value_high, preferred_element_type=F32)


def kernel(
    count, primal, width, face_s, prim_s, face_hbm, prim_hbm, slot_hbm, k_hbm, f_hbm, cinv_hbm, pre_ref, kph_ref, kpl_ref, q_ref, lam_ref,
    face_v, prim_v, slot_v, f_ref, cinv_ref, in_sem, k_ref, kh_ref, kl_ref, e_ref, fh_ref, fl_ref, ks_ref, first_ref, ah_ref, al_ref, cols_ref, ch_ref, cl_ref,
    gat_ref, r_ref, send_r, send_l, got_r, got_l, send_ar, send_al, got_ar, got_al,
    k_sem, send_sem, block_sem, face_sem, cinv_send, cinv_recv, a_send, a_recv,
):
    outer, inner = grid_of(count)
    order, columns = f_ref.shape
    owned = primal // 2
    tile = order // k_sem.shape[0]
    padded = e_ref.shape[1]
    me = lax.axis_index("sub")
    core = lax.rem(me, 2)
    y = lax.rem(me // 2, inner)
    z = me // (2 * inner)

    def at(z_, y_, core_):
        return (z_ * inner + y_) * 2 + core_

    def around(steps):
        return lax.rem(me + (steps + count), count)

    def k_copy(c):
        rows = pl.ds(c * tile, tile)
        return pltpu.make_async_copy(k_hbm.at[rows, :], k_ref.at[rows, :], k_sem.at[c])

    held = [
        pltpu.make_async_copy(src, dst, in_sem.at[i])
        for i, (src, dst) in enumerate((
            (f_hbm, f_ref), (cinv_hbm, cinv_ref), (face_hbm, face_v), (prim_hbm, prim_v), (slot_hbm, slot_v)
        ))
    ]
    for copy in held:
        copy.start()
    for c in range(k_sem.shape[0]):
        k_copy(c).start()

    outer_peers = [at(flipped(z, m, outer), y, core) for m in range(1, outer)]
    outer_back = [returned(z, m, outer) for m in range(1, outer)]
    inner_peers = [at(z, flipped(y, m, inner), core) for m in range(1, inner)]
    partner = at(z, y, 1 - core)
    ring = [around(d) for d in (-1, 1)]

    barrier = pltpu.get_barrier_semaphore()
    greeted = outer_peers + inner_peers + [partner] + ring
    if outer & (outer - 1):
        greeted = greeted + [at(b, y, core) for b in outer_back]
    for peer in greeted:
        pl.semaphore_signal(barrier, inc=1, device_id={"sub": peer}, device_id_type=MESH)

    def remote(src, dst, ssem, rsem, peer):
        return pltpu.make_async_remote_copy(
            src_ref=src, dst_ref=dst, send_sem=ssem, recv_sem=rsem, device_id={"sub": peer}, device_id_type=MESH
        )

    cinv_copies = [
        remote(cinv_ref, cols_ref.at[slot], cinv_send.at[slot], cinv_recv.at[slot], around(d))
        for slot, d in ((0, 1), (1, -1))
    ]
    passed_on = remote(cols_ref.at[1], cols_ref.at[2], cinv_send.at[2], cinv_recv.at[2], around(-1))

    for copy in held:
        copy.wait()

    square = (primal, primal)
    eye = lax.broadcasted_iota(jnp.int32, square, 0) == lax.broadcasted_iota(jnp.int32, square, 1)
    prim_col = jnp.sum(jnp.where(eye, prim_v[...].astype(F32), 0.0), axis=1, keepdims=True)
    slot_col = jnp.sum(jnp.where(eye, slot_v[...].astype(F32), 0.0), axis=1, keepdims=True)
    corner_width = padded - 2 * width
    lane = lax.broadcasted_iota(jnp.int32, (primal, corner_width), 1).astype(F32)
    ordered = jnp.sum(jnp.where(slot_col == lane, prim_col + 1.0, 0.0), axis=0, keepdims=True) - 1.0
    ordering = jnp.where(lax.broadcasted_iota(jnp.int32, square, 0) == slot_v[...], 1.0, 0.0).astype(BF16)

    fh, fl = split(f_ref[...])
    fh_ref[...] = fh
    fl_ref[...] = fl

    def stream(first_tile, last_tile):
        @pl.loop(first_tile, last_tile)
        def _(c):
            k_copy(c).wait()
            rows = pl.ds(pl.multiple_of(c * tile, tile), tile)
            high, low = split(k_ref[rows, :])
            kh_ref[rows, :] = high
            kl_ref[rows, :] = low
            pre_ref[rows, :] = product_parts(high, low, fh_ref[...], fl_ref[...])

    half = 1
    stream(0, half)
    pl.semaphore_wait(barrier, len(greeted))
    for copy in cinv_copies:
        copy.start()
    stream(half, order // tile)

    used = 2 * width + primal

    def picked(to_ref, from_ref):
        def rows_of(start, size, row_at):
            @pl.loop(0, size // 8)
            def _(i):
                base = pl.multiple_of(i * 8, 8)
                for j in range(8):
                    to_ref[pl.ds(start + base + j, 1), :] = from_ref[pl.ds(row_at(base + j), 1), :]

        rows_of(0, width, lambda i: face_s[0, 1, i])
        rows_of(width, width, lambda i: face_s[0, 0, i])
        rows_of(2 * width, primal, lambda i: prim_s[0, i])

    def in_order(value):
        high, low = split(value)
        half_width = value.shape[1]
        both = jnp.dot(ordering, jnp.concatenate([high, low], axis=1), preferred_element_type=F32)
        return both[:, :half_width] + both[:, half_width:]

    picked(first_ref, pre_ref)
    empty = jnp.zeros((padded - used, columns), F32)
    first = jnp.concatenate([first_ref[:2 * width], in_order(first_ref[2 * width:used]), empty], axis=0)

    def one_hot_columns():
        right_ids, left_ids = face_v[0, 1:2, :], face_v[0, 0:1, :]
        ordered_ids = ordered.astype(jnp.int32)

        @pl.loop(0, order // tile)
        def _(c):
            rows = pl.ds(pl.multiple_of(c * tile, tile), tile)
            near = lax.broadcasted_iota(jnp.int32, (tile, width), 0) + c * tile
            e_ref[rows, :width] = jnp.where(near == right_ids, 1.0, 0.0).astype(BF16)
            e_ref[rows, width:2 * width] = jnp.where(near == left_ids, 1.0, 0.0).astype(BF16)
            near = lax.broadcasted_iota(jnp.int32, (tile, corner_width), 0) + c * tile
            e_ref[rows, 2 * width:] = jnp.where(near == ordered_ids, 1.0, 0.0).astype(BF16)

    def finish_a():
        one_hot_columns()
        if padded > used:
            ks_ref[used:, :] = jnp.zeros((padded - used, order), F32)
        picked(ks_ref, k_ref)
        high, low = split(ks_ref[...])
        parts = []
        for part, out in ((high, ah_ref), (low, al_ref)):
            found = jnp.dot(part, e_ref[...], preferred_element_type=F32)
            out[:2 * width, :] = found[:2 * width].astype(BF16)
            out[2 * width:used, :] = jnp.dot(
                ordering, found[2 * width:used].astype(BF16), preferred_element_type=F32
            ).astype(BF16)
            if padded > used:
                out[used:, :] = jnp.zeros((padded - used, padded), BF16)
            parts.append(found[:2 * width, 2 * width:])
        corner = parts[0] + parts[1]
        send_ar[...] = corner[:width]
        send_al[...] = corner[width:]

    def primal_columns():
        picks = e_ref[:, 2 * width:]

        @pl.loop(0, order // tile)
        def _(c):
            rows = pl.ds(pl.multiple_of(c * tile, tile), tile)
            kph_ref[rows, :] = jnp.dot(kh_ref[rows, :], picks, preferred_element_type=F32).astype(BF16)
            kpl_ref[rows, :] = jnp.dot(kl_ref[rows, :], picks, preferred_element_type=F32).astype(BF16)

    def uncorrected(changes):
        high, low = split(changes)
        spread = jnp.dot(e_ref[:, :2 * width], jnp.concatenate([high, low], axis=1), preferred_element_type=F32)
        loads = f_ref[...] + (spread[:, :columns] + spread[:, columns:])
        high, low = split(loads)
        fh_ref[...] = high
        fl_ref[...] = low

        @pl.loop(0, order // tile)
        def _(c):
            rows = pl.ds(pl.multiple_of(c * tile, tile), tile)
            pre_ref[rows, :] = product_parts(kh_ref[rows, :], kl_ref[rows, :], fh_ref[...], fl_ref[...])

    a_copies = [
        remote(send_al, got_al, a_send.at[0], a_recv.at[0], around(-1)),
        remote(send_ar, got_ar, a_send.at[1], a_recv.at[1], around(1)),
    ]

    lam = jnp.zeros((width, columns), F32)
    lam_before = jnp.zeros((width, columns), F32)
    values = first
    changes = None
    for step in range(ITERS):
        if step:
            changes = jnp.concatenate([-lam, lam_before], axis=0)
            values = first + product(ah_ref[:, :2 * width], al_ref[:, :2 * width], changes)
        gat = gat_ref.at[step]
        gat_ref[step, me] = values[2 * width:2 * width + primal]
        send_r[step] = values[:width]
        send_l[step] = values[width:2 * width]
        started = []

        def forward(block, peer, part):
            rows = gat.at[block, pl.ds(part * owned, owned)]
            copy = remote(rows, rows, send_sem.at[step, len(started)], block_sem.at[step, block, part], peer)
            copy.start()
            started.append(copy)

        def arrived(block, part):
            rows = gat.at[block, pl.ds(part * owned, owned)]
            remote(rows, rows, send_sem.at[step, 0], block_sem.at[step, block, part], partner).wait_recv()

        for part in range(2):
            for peer in reversed(outer_peers):
                forward(me, peer, part)
            for peer in inner_peers:
                forward(me, peer, part)
            forward(me, partner, part)
        faces = [
            remote(send_l.at[step], got_l.at[step], face_sem.at[0, step, 0], face_sem.at[1, step, 0], around(-1)),
            remote(send_r.at[step], got_r.at[step], face_sem.at[0, step, 1], face_sem.at[1, step, 1], around(1)),
        ]
        for copy in faces:
            copy.start()

        if step == 0:
            cinv_copies[1].wait_recv()
            passed_on.start()
            finish_a()
            for copy in a_copies:
                copy.start()
        if step == 1:
            primal_columns()
        if step == ITERS - 1:
            uncorrected(changes)

        for part in range(2):
            for source in outer_back:
                block = at(source, y, core)
                arrived(block, part)
                for peer in inner_peers:
                    forward(block, peer, part)
                forward(block, partner, part)
        if step == 0:
            cinv_copies[0].wait()
            cinv_copies[1].wait_send()
            passed_on.wait()
            for slot, part in enumerate((cols_ref.at[0], cinv_ref, cols_ref.at[1], cols_ref.at[2])):
                high, low = split(part[...])
                ch_ref[slot * owned:(slot + 1) * owned, :] = high
                cl_ref[slot * owned:(slot + 1) * owned, :] = low
        for part in range(2):
            for m in range(1, inner):
                for source in [z] + outer_back:
                    block = at(source, returned(y, m, inner), core)
                    arrived(block, part)
                    forward(block, partner, part)
        for part in range(2):
            for source in [z] + outer_back:
                for m in range(inner):
                    arrived(at(source, y if m == 0 else returned(y, m, inner), 1 - core), part)

        for s in range(count):
            r_ref[s * owned:(s + 1) * owned, :] = (
                gat_ref[step, s, :owned, :] + gat_ref[step, (s - 1) % count, owned:, :]
            )
        coarse = product(ch_ref[...], cl_ref[...], r_ref[...])
        fill = jnp.zeros((padded - 2 * width - primal, columns), F32)

        def steps_of(slot):
            return jnp.concatenate([coarse[slot * owned:(slot + 2) * owned], fill], axis=0)

        q_before, q_own, q_after = steps_of(0), steps_of(1), steps_of(2)
        own = product(ah_ref[:2 * width, 2 * width:], al_ref[:2 * width, 2 * width:], q_own)
        if step == 0:
            for copy in a_copies:
                copy.wait()
        for copy in faces:
            copy.wait()
        after = product(*split(got_al[...]), q_after)
        lam = lam + DAMPING * ((values[:width] - own[:width]) - (got_l[step] - after))
        if step + 1 < ITERS:
            before = product(*split(got_ar[...]), q_before)
            lam_before = lam_before + DAMPING * ((got_r[step] - before) - (values[width:2 * width] - own[width:]))
        else:
            lam_ref[...] = lam
            q_ref[...] = q_own
        for copy in started:
            copy.wait_send()


def finish(pre_ref, kph_ref, kpl_ref, q_ref, lam_ref, u_ref, lam_out):
    u_ref[...] = pre_ref[...] - product(kph_ref[...], kpl_ref[...], q_ref[...])
    lam_out[...] = lam_ref[...]


def local(condensed, eigen_loads, coarse_inverse, face_rows, primal_rows, primal_slot):
    count = lax.axis_size("sub")
    order, columns = eigen_loads.shape
    owned, total = coarse_inverse.shape
    width = face_rows.shape[2]
    primal = primal_rows.shape[1]
    padded = 2 * width + -(-primal // LANES) * LANES
    outer, inner = grid_of(count)
    corner_width = padded - 2 * width
    tile = 256 if order % 256 == 0 else order
    sends = (outer - 1) + (inner - 1) * outer + outer * inner
    dma = pltpu.SemaphoreType.DMA
    vmem = pl.BlockSpec(memory_space=pltpu.VMEM)
    face = pltpu.VMEM((ITERS, width, columns), F32)
    corner = pltpu.VMEM((width, padded - 2 * width), F32)
    smem = pl.BlockSpec(memory_space=pltpu.SMEM)
    needed = 8 * order * (order + padded + 2 * columns) + 4 * padded * (order + columns + padded)
    needed += 4 * owned * total * 8 + 4 * columns * (ITERS * (count * primal + 4 * width) + total)
    needed += 4 * order * (columns + 2 * corner_width) + 4 * columns * (order + 8 * width)
    shape = jax.ShapeDtypeStruct
    held = [
        pltpu.with_memory_space_constraint(value, pltpu.HBM)
        for value in (face_rows, primal_rows, primal_slot, condensed, eigen_loads, coarse_inverse)
    ]
    parts = pl.pallas_call(
        functools.partial(kernel, count, primal, width),
        out_shape=(
            shape((order, columns), F32),
            shape((order, corner_width), BF16),
            shape((order, corner_width), BF16),
            shape((corner_width, columns), F32),
            shape((width, columns), F32),
        ),
        in_specs=[smem, smem] + [pl.BlockSpec(memory_space=pltpu.HBM)] * 6,
        out_specs=(vmem,) * 5,
        scratch_shapes=[
            pltpu.VMEM(face_rows.shape, jnp.int32),
            pltpu.VMEM(primal_rows.shape, jnp.int32),
            pltpu.VMEM(primal_slot.shape, jnp.int32),
            pltpu.VMEM((order, columns), F32),
            pltpu.VMEM((owned, total), F32),
            dma((5,)),
            pltpu.VMEM((order, order), F32),
            pltpu.VMEM((order, order), BF16),
            pltpu.VMEM((order, order), BF16),
            pltpu.VMEM((order, padded), BF16),
            pltpu.VMEM((order, columns), BF16),
            pltpu.VMEM((order, columns), BF16),
            pltpu.VMEM((padded, order), F32),
            pltpu.VMEM((padded, columns), F32),
            pltpu.VMEM((padded, padded), BF16),
            pltpu.VMEM((padded, padded), BF16),
            pltpu.VMEM((3, owned, total), F32),
            pltpu.VMEM((4 * owned, total), BF16),
            pltpu.VMEM((4 * owned, total), BF16),
            pltpu.VMEM((ITERS, count, primal, columns), F32),
            pltpu.VMEM((total, columns), F32),
            face, face, face, face,
            corner, corner, corner, corner,
            dma((order // tile,)),
            dma((ITERS, 2 * sends)),
            dma((ITERS, count, 2)),
            dma((2, ITERS, 2)),
            dma((3,)),
            dma((3,)),
            dma((2,)),
            dma((2,)),
        ],
        compiler_params=pltpu.CompilerParams(
            collective_id=0, has_side_effects=True, vmem_limit_bytes=min(VMEM_LIMIT, needed + needed // 4)
        ),
    )(face_rows, primal_rows, *held)
    return pl.pallas_call(
        finish,
        out_shape=(shape((order, columns), F32), shape((width, columns), F32)),
        in_specs=[vmem] * 5,
        out_specs=(vmem, vmem),
        compiler_params=pltpu.CompilerParams(vmem_limit_bytes=4 * order * columns * 8),
    )(*parts)


def solution(mesh):
    placed = (
        P(("rve", "sub"), None),
        P(("rve", "sub"), None),
        P(("rve", "sub"), None),
        P("sub", None, None),
        P("sub", None),
        P("sub", None),
    )
    return jax.shard_map(
        local,
        mesh=mesh,
        in_specs=placed,
        out_specs=(P(("rve", "sub"), None), P(("rve", "sub"), None)),
        check_vma=False,
    )
```
